512 devices in a mesh: row: 16 (over z, y_lo), col: 8 (over y_hi, core), rep: 4 (over x).
Axes of the slice: x: 4, y: 8 (y_hi: 4, y_lo: 2; y = y_hi * 2 + y_lo), z: 8, core: 2. Of those that a mesh axis runs over, the one named last changes fastest.
Arguments:
- genotypes: bfloat16 [2048, 16384], P(('row', 'col', 'rep')), may hold values from 0 to 2, as said below
Outputs:
- main_tiles: float32 [16, 8, 1024, 1024], P('row', 'col', 'rep')
- half_tiles: float32 [16, 1024, 1024], P('row', 'rep', 'col')
The draws below stay inside these ranges and needn't reach their ends.
Inputs may be any that keep to these rules, and one draw needn't show every extreme that they name: `genotypes`: imputed dosages of the alternate allele, real-valued.
All inputs are finite; a program needn't handle non-finite values.
Results may differ from the reference program's by a relative error of at most 0.008.
Values may be sent and summed in bfloat16 or wider, within the bound.
No kernel may reach another device: no remote copies, remote signals or barrier semaphores. Data moves between devices by JAX's collectives and lax.ppermute only.
A program may use at most 64 MiB of HBM per device.

```python
import jax
import jax.numpy as jnp
from jax import lax

VARIANTS = 16384
ROWS_DEV = 4
BLOCKS = 16
BLOCK_W = 1024
SAMPLES = 2048
N_ROW = 16
N_COL = 8
N_REP = 4


def draw_genotypes(key, part):
    key_rate = jax.random.fold_in(key, 11)
    key_first = jax.random.fold_in(key, 12)
    key_second = jax.random.fold_in(key, 13)
    rate = jax.random.uniform(key_rate, (1, VARIANTS), jnp.float32, 0.05, 0.6)
    sample_pos = jnp.arange(SAMPLES, dtype=jnp.float32)[:, None]
    trend = (SAMPLES + 2.0 * sample_pos) / (3.0 * SAMPLES)
    first_draw = jax.random.uniform(key_first, (SAMPLES, VARIANTS), jnp.float32, 0.0, 1.0)
    second_draw = jax.random.uniform(key_second, (SAMPLES, VARIANTS), jnp.float32, 0.0, 1.0)
    first_allele = jnp.minimum(1.0, 2.0 * rate * trend * first_draw)
    second_allele = jnp.minimum(1.0, 2.0 * rate * trend * second_draw)
    return (first_allele + second_allele).astype(jnp.bfloat16)


def setup_inputs(seed: int = 0) -> dict:
    arg_keys = jax.random.split(jax.random.key(seed), 2)
    genotypes = draw_genotypes(jax.random.fold_in(arg_keys[1], 71), 0)
    return {"genotypes": genotypes}


def reference(genotypes):
    dosage = genotypes.astype(jnp.float32)
    sample_count = dosage.shape[0]
    sum_dose = lax.optimization_barrier(jnp.sum(dosage, axis=0))
    sum_square = lax.optimization_barrier(jnp.sum(dosage * dosage, axis=0))
    average = sum_dose / sample_count
    spread = sum_square / sample_count - average * average
    scaled = ((dosage - average) * lax.rsqrt(spread + 1e-05)).astype(jnp.bfloat16)
    grouped = scaled.reshape(N_ROW * N_COL, N_REP, ROWS_DEV, VARIANTS)
    tile_width = (N_COL + 1) * BLOCK_W
    replica_list = []
    for replica in range(N_REP):
        replica_rows = grouped[:, replica].reshape(-1, VARIANTS).astype(jnp.float32)
        replica_list.append((replica_rows, jnp.concatenate([replica_rows, replica_rows], axis=1)))

    def one_row(block_index):
        running = jnp.zeros((BLOCK_W, tile_width), jnp.float32)
        begin = (block_index * BLOCK_W).astype(jnp.int32)
        for replica_rows, doubled in replica_list:
            left_cols = lax.dynamic_slice_in_dim(replica_rows, begin, BLOCK_W, 1)
            right_cols = lax.dynamic_slice_in_dim(doubled, begin, tile_width, 1)
            portion = jnp.dot(left_cols.T, right_cols, preferred_element_type=jnp.float32, precision=lax.Precision.HIGHEST) * (1.0 / SAMPLES)
            rounded = lax.optimization_barrier(portion.astype(jnp.bfloat16))
            running = running + rounded.astype(jnp.float32)
        return running.reshape(BLOCK_W, N_COL + 1, BLOCK_W).transpose(1, 0, 2)
    all_tiles = lax.map(one_row, jnp.arange(BLOCKS, dtype=jnp.int32))
    return (all_tiles[:, :N_COL], all_tiles[:, N_COL])
```

```python
import functools

import jax
import jax.numpy as jnp
from jax import lax
from jax.experimental import pallas as pl
from jax.experimental.pallas import tpu as pltpu
from jax.sharding import PartitionSpec as P

F32 = jnp.float32
BF16 = jnp.bfloat16
EPS = 1e-05


def thirds(v):
    hi = v.astype(BF16).astype(F32)
    rest = v - hi
    mid = rest.astype(BF16).astype(F32)
    return hi, mid, (rest - mid).astype(BF16).astype(F32)


def pack_body(n_row, n_col, x_ref, out_ref):
    width = x_ref.shape[1] // n_row
    half, slab = width // 2, width // n_col
    for r in range(n_row):
        for c in range(n_col):
            d = r * n_col + c
            near = r * width + (c % 2) * half
            pair = ((r + c) % n_row) * width
            far = ((r + n_row // 2) % n_row) * width + c * slab
            out_ref[d, :, :half] = x_ref[:, near : near + half]
            out_ref[d, :, half : half + width] = x_ref[:, pair : pair + width]
            out_ref[d, :, half + width :] = x_ref[:, far : far + slab]


def sums(v):
    v = v.astype(F32)
    return jnp.sum(v, axis=0, keepdims=True), jnp.sum(v * v, axis=0, keepdims=True)


def tile_body(n_rep, own_ref, other_ref, out_ref):
    samples, half = other_ref.shape
    sub = 2 * half // n_rep
    core = lax.rem(lax.axis_index("col"), 2)
    right = own_ref[:, half:]
    cols = right.shape[1]
    dose, square = sums(right)
    hi, mid, lo = thirds(dose)
    fold = -1.0 / samples
    pad = jnp.zeros((2, cols), F32)
    right_fix = (jnp.concatenate([hi, mid, hi, mid, lo, hi, pad], axis=0) * fold).astype(BF16)
    mean = dose / samples
    col_rows = [*thirds(mean), *thirds(square - dose * mean)]
    per_half = n_rep // 2
    for side, ref in enumerate((own_ref, other_ref)):
        for j in range(per_half):
            left = ref[:, j * sub : (j + 1) * sub]
            l_dose, l_square = sums(left)
            hi, mid, lo = thirds(l_dose)
            pad = jnp.zeros((2, sub), F32)
            left_fix = jnp.concatenate([hi, hi, mid, mid, hi, lo, pad], axis=0).astype(BF16)
            part = lax.dot_general(left, right, (((0,), (0,)), ((), ())), preferred_element_type=F32)
            part += lax.dot_general(left_fix, right_fix, (((0,), (0,)), ((), ())), preferred_element_type=F32)
            l_mean = l_dose / samples
            gap = jnp.zeros((1, cols - 3 * sub), F32)
            rows = [
                jnp.concatenate([*thirds(l_mean), gap], axis=1),
                jnp.concatenate([*thirds(l_square - l_dose * l_mean), gap], axis=1),
            ]
            to = lax.rem(per_half * (side + core), n_rep) + j
            out_ref[to, :sub, :] = part.astype(BF16)
            out_ref[to, sub:, :] = jnp.concatenate(col_rows + rows, axis=0).astype(BF16)


def whole(means, squares, samples):
    count = len(means)
    mean = sum(means) / count
    off = [m - mean for m in means]
    spread = sum(squares) / (count * samples) + sum(o * o for o in off) / count
    return off, lax.rsqrt(spread + EPS)


def join_body(samples, in_ref, main_ref, half_ref):
    n_rep, rows, cols = in_ref.shape
    sub = rows - 8
    width = main_ref.shape[1]
    total = sum(in_ref[q, :sub, :].astype(F32) for q in range(n_rep))
    stats = [in_ref[q, sub:, :].astype(F32) for q in range(n_rep)]
    three = lambda s, i: s[i : i + 1] + s[i + 1 : i + 2] + s[i + 2 : i + 3]
    flat = lambda s, i: s[i : i + 1, :sub] + s[i : i + 1, sub : 2 * sub] + s[i : i + 1, 2 * sub : 3 * sub]
    off, scale = whole([three(s, 0) for s in stats], [three(s, 3) for s in stats], samples)
    l_off, l_scale = whole([flat(s, 6) for s in stats], [flat(s, 7) for s in stats], samples)
    pad = [jnp.zeros((1, sub), F32)] * (7 - n_rep)
    turned = jnp.concatenate(l_off + [l_scale / (n_rep * samples)] + pad, axis=0).T
    for q in range(n_rep):
        total += (turned[:, q : q + 1] * samples) * off[q]
    total = total * turned[:, n_rep : n_rep + 1] * scale
    main_ref[...] = total[:, :width]
    half_ref[...] = total[:, width:]


def body(genotypes):
    sample_rows, variants = genotypes.shape
    n_row, n_col, n_rep = (lax.axis_size(a) for a in ("row", "col", "rep"))
    width = variants // n_row
    half, slab = width // 2, width // n_col
    pairs = n_row * n_col
    samples = sample_rows * pairs
    wide = half + width + slab
    cols = width + slab
    sub = width // n_rep
    payload = pl.pallas_call(
        functools.partial(pack_body, n_row, n_col),
        out_shape=jax.ShapeDtypeStruct((pairs, sample_rows, wide), BF16),
        name="pack",
    )(genotypes)
    arrived = lax.all_to_all(payload, ("row", "col"), 0, 0, tiled=True)
    swap = [(c, c ^ 1) for c in range(n_col)]
    other = lax.ppermute(arrived[:, :, :half], "col", swap)
    partial = pl.pallas_call(
        functools.partial(tile_body, n_rep),
        out_shape=jax.ShapeDtypeStruct((n_rep, sub + 8, cols), BF16),
        name="tile",
    )(arrived.reshape(samples, wide), other.reshape(samples, half))
    parts = lax.all_to_all(partial, "rep", 0, 0, tiled=True)
    main, far = pl.pallas_call(
        functools.partial(join_body, samples),
        out_shape=(jax.ShapeDtypeStruct((sub, width), F32), jax.ShapeDtypeStruct((sub, slab), F32)),
        name="join",
    )(parts)
    return main.reshape(1, 1, sub, width), far.reshape(1, sub, slab)


def solution(mesh):
    return jax.shard_map(
        body,
        mesh=mesh,
        in_specs=(P(("row", "col", "rep"), None),),
        out_specs=(P("row", "col", "rep", None), P("row", "rep", "col")),
        check_vma=False,
    )
```

```python
import functools

import jax
import jax.numpy as jnp
from jax import lax
from jax.experimental import pallas as pl
from jax.experimental.pallas import tpu as pltpu
from jax.sharding import PartitionSpec as P


F32 = jnp.float32
BF16 = jnp.bfloat16
EPS = 1e-05


def params(mib):
    return pltpu.CompilerParams(vmem_limit_bytes=mib << 20)


def cost(flops, size):
    return pl.CostEstimate(flops=flops, bytes_accessed=size, transcendentals=0)


def thirds(v):
    hi = v.astype(BF16).astype(F32)
    rest = v - hi
    mid = rest.astype(BF16).astype(F32)
    return hi, mid, (rest - mid).astype(BF16).astype(F32)


def sums(v):
    v = v.astype(F32)
    return jnp.sum(v, axis=0, keepdims=True), jnp.sum(v * v, axis=0, keepdims=True)


def stacked(rows, count):
    gap = jnp.zeros((count - len(rows), rows[0].shape[1]), F32)
    return jnp.concatenate([*rows, gap], axis=0)


def dot0(a, b):
    return lax.dot_general(a, b, (((0,), (0,)), ((), ())), preferred_element_type=F32)


def pack_first(n_row, n_col, x_ref, out_ref):
    width = x_ref.shape[1] // n_row
    half, slab = width // 2, width // n_col
    for r in range(n_row):
        for c in range(n_col):
            d = r * n_col + c
            near = r * width + (c % 2) * half
            pair = ((r + c) % n_row) * width
            far = ((r + n_row // 2) % n_row) * width + c * slab
            out_ref[d, :, :half] = x_ref[:, near : near + half]
            out_ref[d, :, half : 2 * half] = x_ref[:, pair : pair + half]
            out_ref[d, :, 2 * half :] = x_ref[:, far : far + slab]


def pack_second(n_row, n_col, x_ref, out_ref):
    width = x_ref.shape[1] // n_row
    half = width // 2
    for r in range(n_row):
        for c in range(n_col):
            pair = ((r + c) % n_row) * width + half
            out_ref[r * n_col + c] = x_ref[:, pair : pair + half]


def column_side(right):
    samples = right.shape[0]
    dose, square = sums(right)
    hi, mid, lo = thirds(dose)
    fix = (stacked([hi, mid, hi, mid, lo, hi], 8) * (-1.0 / samples)).astype(BF16)
    mean = dose / samples
    return fix, [*thirds(mean), *thirds(square - dose * mean)]


def tile_first(n_rep, own_ref, other_ref, left_ref, fix_ref, *out_refs):
    samples, half = other_ref.shape
    sub = 2 * half // n_rep
    core = lax.rem(lax.axis_index("col"), 2)
    group = lax.axis_index("rep")
    left_ref[:, pl.ds(pl.multiple_of(core * half, half), half)] = own_ref[:, :half]
    left_ref[:, pl.ds(pl.multiple_of((1 - core) * half, half), half)] = other_ref[...]
    right = own_ref[:, half:]
    cols = right.shape[1]
    right_fix, col_rows = column_side(right)
    gap = jnp.zeros((1, cols - sub), F32)
    for k in range(n_rep):
        at = pl.ds(pl.multiple_of(lax.rem(group + k, n_rep) * sub, sub), sub)
        left = left_ref[:, at]
        dose, square = sums(left)
        hi, mid, lo = thirds(dose)
        left_fix = stacked([hi, hi, mid, mid, hi, lo], 8).astype(BF16)
        fix_ref[:, at] = left_fix
        mean = dose / samples
        rows = [*thirds(mean), *thirds(square - dose * mean)]
        rows = [jnp.concatenate([v, gap], axis=1) for v in rows]
        part = dot0(left, right) + dot0(left_fix, right_fix)
        out_refs[k][:sub, :] = part.astype(BF16)
        out_refs[k][sub:, :] = stacked(col_rows + rows, 16).astype(BF16)


def tile_second(left_ref, fix_ref, right_ref, out_ref):
    n_rep, rows, _ = out_ref.shape
    sub = rows - 8
    right = right_ref[...]
    right_fix, col_rows = column_side(right)
    foot = stacked(col_rows, 8).astype(BF16)
    for q in range(n_rep):
        at = slice(q * sub, (q + 1) * sub)
        part = dot0(left_ref[:, at], right) + dot0(fix_ref[:, at], right_fix)
        out_ref[q, :sub, :] = part.astype(BF16)
        out_ref[q, sub:, :] = foot


def whole(means, squares, samples):
    count = len(means)
    mean = sum(means) / count
    off = [m - mean for m in means]
    spread = sum(squares) / (count * samples) + sum(o * o for o in off) / count
    return off, lax.rsqrt(spread + EPS)


def three(s, i):
    return s[i : i + 1] + s[i + 1 : i + 2] + s[i + 2 : i + 3]


def joined(parts, stats, turned, samples):
    n_rep = len(parts)
    off, scale = whole([three(s, 0) for s in stats], [three(s, 3) for s in stats], samples)
    total = sum(p.astype(F32) for p in parts)
    for q in range(n_rep):
        total += (turned[:, q : q + 1] * samples) * off[q]
    return total * turned[:, n_rep : n_rep + 1] * scale


def join_first(samples, *refs):
    *in_refs, turned_ref, main_ref, half_ref = refs
    n_rep = len(in_refs)
    sub, width = main_ref.shape
    stats = [r[sub:, :].astype(F32) for r in in_refs]
    l_off, l_scale = whole(
        [three(s[:, :sub], 6) for s in stats], [three(s[:, :sub], 9) for s in stats], samples
    )
    turned = stacked(l_off + [l_scale / (n_rep * samples)], 8).T
    total = joined([r[:sub, :] for r in in_refs], stats, turned, samples)
    main_ref[...] = total[:, :width]
    half_ref[...] = total[:, width:]
    group = lax.axis_index("rep")
    line = lax.broadcasted_iota(jnp.int32, (8, sub), 0)
    ordered = jnp.where(line == n_rep, l_scale / (n_rep * samples), 0.0)
    for k in range(n_rep):
        source = lax.rem(group + n_rep - k, n_rep)
        ordered = jnp.where(line == source, l_off[k], ordered)
    turned_ref[...] = ordered.T


def join_second(samples, in_ref, turned_ref, main_in, main_ref):
    n_rep, rows, _ = in_ref.shape
    sub = rows - 8
    stats = [in_ref[q, sub:, :].astype(F32) for q in range(n_rep)]
    parts = [in_ref[q, :sub, :] for q in range(n_rep)]
    main_ref[...] = joined(parts, stats, turned_ref[...], samples)


def steps(genotypes):
    sample_rows, variants = genotypes.shape
    n_row, n_col, n_rep = (lax.axis_size(a) for a in ("row", "col", "rep"))
    width = variants // n_row
    half, slab = width // 2, width // n_col
    pairs = n_row * n_col
    samples = sample_rows * pairs
    cols = half + slab
    sub = width // n_rep
    shape = jax.ShapeDtypeStruct

    def pack(fn, wide):
        return pl.pallas_call(
            functools.partial(fn, n_row, n_col),
            out_shape=shape((pairs, sample_rows, wide), BF16),
            compiler_params=params(8),
            cost_estimate=cost(0, 4 * pairs * sample_rows * wide),
        )(genotypes)

    send_first = pack(pack_first, half + cols)
    send_second = pack(pack_second, half)
    first = lax.all_to_all(send_first, ("row", "col"), 0, 0, tiled=True)
    second = lax.all_to_all(send_second, ("row", "col"), 0, 0, tiled=True)
    swap = [(c, c ^ 1) for c in range(n_col)]
    other = lax.ppermute(first[:, :, :half], "col", swap)
    left, fix, *parts = pl.pallas_call(
        functools.partial(tile_first, n_rep),
        out_shape=(
            shape((samples, width), BF16),
            shape((8, width), BF16),
            *[shape((sub + 16, cols), BF16)] * n_rep,
        ),
        compiler_params=params(16),
        cost_estimate=cost(2 * samples * width * cols, 2 * samples * (2 * width + cols)),
        name="tile_first",
    )(first.reshape(samples, half + cols), other.reshape(samples, half))
    for k in range(1, n_rep):
        parts[k] = lax.ppermute(parts[k], "rep", [(q, (q + k) % n_rep) for q in range(n_rep)])
    turned, main, far = pl.pallas_call(
        functools.partial(join_first, samples),
        grid=(1,),
        in_specs=[pl.BlockSpec((sub + 16, cols), lambda i: (0, 0))] * n_rep,
        out_specs=(
            pl.BlockSpec((sub, 8), lambda i: (0, 0)),
            pl.BlockSpec((sub, half), lambda i: (0, 0)),
            pl.BlockSpec((sub, slab), lambda i: (0, 0)),
        ),
        out_shape=(shape((sub, 8), F32), shape((sub, width), F32), shape((sub, slab), F32)),
        compiler_params=params(8),
        cost_estimate=cost(12 * sub * cols, 12 * sub * cols),
        name="join_first",
    )(*parts)
    partial = pl.pallas_call(
        tile_second,
        out_shape=shape((n_rep, sub + 8, half), BF16),
        compiler_params=params(16),
        cost_estimate=cost(2 * samples * width * half, 2 * samples * (width + half)),
        name="tile_second",
    )(left, fix, second.reshape(samples, half))
    rest = lax.all_to_all(partial, "rep", 0, 0, tiled=True)
    main = pl.pallas_call(
        functools.partial(join_second, samples),
        grid=(1,),
        in_specs=[
            pl.BlockSpec((n_rep, sub + 8, half), lambda i: (0, 0, 0)),
            pl.BlockSpec((sub, 8), lambda i: (0, 0)),
            pl.BlockSpec(memory_space=pl.ANY),
        ],
        out_specs=pl.BlockSpec((sub, half), lambda i: (0, 1)),
        out_shape=shape((sub, width), F32),
        input_output_aliases={2: 0},
        compiler_params=params(8),
        cost_estimate=cost(12 * sub * half, 12 * sub * half),
        name="join_second",
    )(rest, turned, main)
    return main.reshape(1, 1, sub, width), far.reshape(1, sub, slab)


def solution(mesh):
    return jax.shard_map(
        steps,
        mesh=mesh,
        in_specs=(P(("row", "col", "rep"), None),),
        out_specs=(P("row", "col", "rep", None), P("row", "rep", "col")),
        check_vma=False,
    )
```

```python
import functools

import jax
import jax.numpy as jnp
from jax import lax
from jax.experimental import pallas as pl
from jax.experimental.pallas import tpu as pltpu
from jax.sharding import PartitionSpec as P


F32 = jnp.float32
BF16 = jnp.bfloat16
EPS = 1e-05


def params(mib):
    return pltpu.CompilerParams(vmem_limit_bytes=mib << 20)


def cost(flops, size):
    return pl.CostEstimate(flops=flops, bytes_accessed=size, transcendentals=0)


def thirds(v):
    hi = v.astype(BF16).astype(F32)
    rest = v - hi
    mid = rest.astype(BF16).astype(F32)
    return hi, mid, (rest - mid).astype(BF16).astype(F32)


def sums(v):
    v = v.astype(F32)
    return jnp.sum(v, axis=0, keepdims=True), jnp.sum(v * v, axis=0, keepdims=True)


def stacked(rows, count):
    gap = jnp.zeros((count - len(rows), rows[0].shape[1]), F32)
    return jnp.concatenate([*rows, gap], axis=0)


def dot0(a, b):
    return lax.dot_general(a, b, (((0,), (0,)), ((), ())), preferred_element_type=F32)


def pack_body(n_row, n_col, x_ref, out_ref):
    width = x_ref.shape[1] // n_row
    half, slab = width // 2, width // n_col
    for r in range(n_row):
        for c in range(n_col):
            d = r * n_col + c
            near = r * width + (c % 2) * half
            pair = ((r + c) % n_row) * width + (c % 2) * half
            far = ((r + n_row // 2) % n_row) * width + c * slab
            out_ref[d, :, :half] = x_ref[:, near : near + half]
            out_ref[d, :, half : 2 * half] = x_ref[:, pair : pair + half]
            out_ref[d, :, 2 * half :] = x_ref[:, far : far + slab]


def column_side(right):
    samples = right.shape[0]
    dose, square = sums(right)
    hi, mid, lo = thirds(dose)
    fix = (stacked([hi, mid, hi, mid, lo, hi], 8) * (-1.0 / samples)).astype(BF16)
    mean = dose / samples
    return fix, [*thirds(mean), *thirds(square - dose * mean)]


def tile_first(own_ref, other_ref, left_ref, fix_ref, out_ref):
    n_rep, rows, cols = out_ref.shape
    samples, half = other_ref.shape
    sub = rows - 16
    core = lax.rem(lax.axis_index("col"), 2)
    left_ref[:, pl.ds(pl.multiple_of(core * half, half), half)] = own_ref[:, :half]
    left_ref[:, pl.ds(pl.multiple_of((1 - core) * half, half), half)] = other_ref[...]
    right = own_ref[:, own_ref.shape[1] - cols :]
    right_fix, col_rows = column_side(right)
    gap = jnp.zeros((1, cols - sub), F32)
    for q in range(n_rep):
        at = slice(q * sub, (q + 1) * sub)
        left = left_ref[:, at]
        dose, square = sums(left)
        hi, mid, lo = thirds(dose)
        left_fix = stacked([hi, hi, mid, mid, hi, lo], 8).astype(BF16)
        fix_ref[:, at] = left_fix
        mean = dose / samples
        rows_of = [*thirds(mean), *thirds(square - dose * mean)]
        rows_of = [jnp.concatenate([v, gap], axis=1) for v in rows_of]
        part = dot0(left, right) + dot0(left_fix, right_fix)
        out_ref[q, :sub, :] = part.astype(BF16)
        out_ref[q, sub:, :] = stacked(col_rows + rows_of, 16).astype(BF16)


def more_tiles(left_ref, fix_ref, right, out_ref):
    n_rep, rows, _ = out_ref.shape
    sub, cols = rows - 8, right.shape[1]
    right_fix, col_rows = column_side(right)
    foot = stacked(col_rows, 8).astype(BF16)
    for q in range(n_rep):
        at = slice(q * sub, (q + 1) * sub)
        part = dot0(left_ref[:, at], right) + dot0(fix_ref[:, at], right_fix)
        out_ref[q, :sub, :cols] = part.astype(BF16)
        out_ref[q, sub:, :cols] = foot


def tile_second(first_col, left_ref, fix_ref, own_ref, out_ref):
    more_tiles(left_ref, fix_ref, own_ref[:, first_col : first_col + out_ref.shape[2]], out_ref)


def tile_third(left_ref, fix_ref, swapped_ref, second_ref, out_ref):
    cols = swapped_ref.shape[1]
    out_ref[:, :, cols:] = second_ref[...]
    more_tiles(left_ref, fix_ref, swapped_ref[...], out_ref)


def whole(means, squares, samples):
    count = len(means)
    mean = sum(means) / count
    off = [m - mean for m in means]
    spread = sum(squares) / (count * samples) + sum(o * o for o in off) / count
    return off, lax.rsqrt(spread + EPS)


def three(s, i):
    return s[i : i + 1] + s[i + 1 : i + 2] + s[i + 2 : i + 3]


def joined(parts, stats, turned, samples):
    n_rep = len(parts)
    off, scale = whole([three(s, 0) for s in stats], [three(s, 3) for s in stats], samples)
    total = sum(p.astype(F32) for p in parts)
    for q in range(n_rep):
        total += (turned[:, q : q + 1] * samples) * off[q]
    return total * turned[:, n_rep : n_rep + 1] * scale


def join_first(samples, in_ref, turned_ref, near_ref, half_ref):
    n_rep, _, _ = in_ref.shape
    sub, near = near_ref.shape
    stats = [in_ref[q, sub:, :].astype(F32) for q in range(n_rep)]
    l_off, l_scale = whole(
        [three(s[:, :sub], 6) for s in stats], [three(s[:, :sub], 9) for s in stats], samples
    )
    turned = stacked(l_off + [l_scale / (n_rep * samples)], 8).T
    total = joined([in_ref[q, :sub, :] for q in range(n_rep)], stats, turned, samples)
    near_ref[...] = total[:, :near]
    half_ref[...] = total[:, near:]
    turned_ref[...] = turned


def join_second(samples, in_ref, turned_ref, near_ref, main_ref):
    n_rep, _, _ = in_ref.shape
    sub, width = main_ref.shape
    half, near = width // 2, near_ref.shape[1]
    core = lax.rem(lax.axis_index("col"), 2)
    stats = [in_ref[q, sub:, :].astype(F32) for q in range(n_rep)]
    total = joined([in_ref[q, :sub, :] for q in range(n_rep)], stats, turned_ref[...], samples)
    mine = pl.multiple_of(core * half, half)
    main_ref[:, pl.ds(pl.multiple_of((1 - core) * half, half), half)] = total[:, :half]
    main_ref[:, pl.ds(mine, half - near)] = total[:, half:]
    main_ref[:, pl.ds(pl.multiple_of(mine + half - near, 128), near)] = near_ref[...]


def steps(genotypes):
    sample_rows, variants = genotypes.shape
    n_row, n_col, n_rep = (lax.axis_size(a) for a in ("row", "col", "rep"))
    width = variants // n_row
    half, slab = width // 2, width // n_col
    pairs = n_row * n_col
    samples = sample_rows * pairs
    sub = width // n_rep
    cols = half + slab
    near = half // 2
    one, two = near + slab, width - near
    shape = jax.ShapeDtypeStruct

    payload = pl.pallas_call(
        functools.partial(pack_body, n_row, n_col),
        out_shape=shape((pairs, sample_rows, half + cols), BF16),
        compiler_params=params(8),
        cost_estimate=cost(0, 4 * pairs * sample_rows * (half + cols)),
        name="pack",
    )(genotypes)
    arrived = lax.all_to_all(payload, ("row", "col"), 0, 0, tiled=True)

    def mate(r, c):
        return ((r - 1) % n_row) * n_col + c + 1 if c % 2 == 0 else ((r + 1) % n_row) * n_col + c - 1

    mates = [(r * n_col + c, mate(r, c)) for r in range(n_row) for c in range(n_col)]
    swapped = lax.ppermute(arrived[:, :, half : 2 * half], ("row", "col"), mates)
    other = lax.ppermute(arrived[:, :, :half], "col", [(c, c ^ 1) for c in range(n_col)])
    own = arrived.reshape(samples, half + cols)
    left, fix, part_one = pl.pallas_call(
        tile_first,
        out_shape=(
            shape((samples, width), BF16),
            shape((8, width), BF16),
            shape((n_rep, sub + 16, one), BF16),
        ),
        compiler_params=params(16),
        cost_estimate=cost(2 * samples * width * one, 2 * samples * (2 * width + one)),
        name="tile_first",
    )(own, other.reshape(samples, half))
    got_one = lax.all_to_all(part_one, "rep", 0, 0, tiled=True)
    part_two = pl.pallas_call(
        functools.partial(tile_second, half),
        out_shape=shape((n_rep, sub + 8, half - near), BF16),
        compiler_params=params(16),
        cost_estimate=cost(2 * samples * width * (half - near), 2 * samples * 2 * width),
        name="tile_second",
    )(left, fix, own)
    part_two = pl.pallas_call(
        tile_third,
        out_shape=shape((n_rep, sub + 8, two), BF16),
        compiler_params=params(16),
        cost_estimate=cost(2 * samples * width * half, 2 * samples * (width + half)),
        name="tile_third",
    )(left, fix, swapped.reshape(samples, half), part_two)
    got_two = lax.all_to_all(part_two, "rep", 0, 0, tiled=True)
    turned, near_main, far = pl.pallas_call(
        functools.partial(join_first, samples),
        out_shape=(shape((sub, 8), F32), shape((sub, near), F32), shape((sub, slab), F32)),
        compiler_params=params(8),
        cost_estimate=cost(12 * sub * one, 12 * sub * one),
        name="join_first",
    )(got_one)
    main = pl.pallas_call(
        functools.partial(join_second, samples),
        out_shape=shape((sub, width), F32),
        compiler_params=params(8),
        cost_estimate=cost(12 * sub * two, 12 * sub * two),
        name="join_second",
    )(got_two, turned, near_main)
    return main.reshape(1, 1, sub, width), far.reshape(1, sub, slab)


def solution(mesh):
    return jax.shard_map(
        steps,
        mesh=mesh,
        in_specs=(P(("row", "col", "rep"), None),),
        out_specs=(P("row", "col", "rep", None), P("row", "rep", "col")),
        check_vma=False,
    )
```

```python
import functools

import jax
import jax.numpy as jnp
from jax import lax
from jax.experimental import pallas as pl
from jax.experimental.pallas import tpu as pltpu
from jax.sharding import PartitionSpec as P


F32 = jnp.float32
BF16 = jnp.bfloat16
EPS = 1e-05
NEAR = 4


def params(mib):
    return pltpu.CompilerParams(vmem_limit_bytes=mib << 20)


def cost(flops, size):
    return pl.CostEstimate(flops=flops, bytes_accessed=size, transcendentals=0)


def thirds(v):
    hi = v.astype(BF16).astype(F32)
    rest = v - hi
    mid = rest.astype(BF16).astype(F32)
    return hi, mid, (rest - mid).astype(BF16).astype(F32)


def sums(v):
    v = v.astype(F32)
    return jnp.sum(v, axis=0, keepdims=True), jnp.sum(v * v, axis=0, keepdims=True)


def stacked(rows, count):
    gap = jnp.zeros((count - len(rows), rows[0].shape[1]), F32)
    return jnp.concatenate([*rows, gap], axis=0)


def dot0(a, b):
    return lax.dot_general(a, b, (((0,), (0,)), ((), ())), preferred_element_type=F32)


def pack_body(n_row, n_col, x_ref, out_ref):
    width = x_ref.shape[1] // n_row
    half, slab = width // 2, width // n_col
    for r in range(n_row):
        for c in range(n_col):
            d = r * n_col + c
            near = r * width + (c % 2) * half
            pair = ((r + c) % n_row) * width + (c % 2) * half
            far = ((r + n_row // 2) % n_row) * width + c * slab
            out_ref[d, :, :half] = x_ref[:, near : near + half]
            out_ref[d, :, half : 2 * half] = x_ref[:, pair : pair + half]
            out_ref[d, :, 2 * half :] = x_ref[:, far : far + slab]


def split_body(in_ref, pair_ref, core_ref, own_ref):
    half = pair_ref.shape[2]
    core_ref[...] = in_ref[:, :, :half]
    pair_ref[...] = in_ref[:, :, half : 2 * half]
    own_ref[...] = in_ref[...].reshape(own_ref.shape)


def column_side(right):
    samples = right.shape[0]
    dose, square = sums(right)
    hi, mid, lo = thirds(dose)
    fix = (stacked([hi, mid, hi, mid, lo, hi], 8) * (-1.0 / samples)).astype(BF16)
    mean = dose / samples
    return fix, [*thirds(mean), *thirds(square - dose * mean)]


def tile_first(own_ref, other_ref, left_ref, fix_ref, *out_refs):
    n_rep = len(out_refs)
    rows, cols = out_refs[0].shape
    samples, half = own_ref.shape[0], other_ref.shape[2]
    sub = rows - 16
    core = lax.rem(lax.axis_index("col"), 2)
    group = lax.axis_index("rep")
    left_ref[:, pl.ds(pl.multiple_of(core * half, half), half)] = own_ref[:, :half]
    left_ref[:, pl.ds(pl.multiple_of((1 - core) * half, half), half)] = other_ref[...].reshape(samples, half)
    right = own_ref[:, own_ref.shape[1] - cols :]
    right_fix, col_rows = column_side(right)
    gap = [jnp.zeros((1, cols - sub), F32)] if cols > sub else []
    for k in range(n_rep):
        at = pl.ds(pl.multiple_of(lax.rem(group + k, n_rep) * sub, sub), sub)
        left = left_ref[:, at]
        dose, square = sums(left)
        hi, mid, lo = thirds(dose)
        left_fix = stacked([hi, hi, mid, mid, hi, lo], 8).astype(BF16)
        fix_ref[:, at] = left_fix
        mean = dose / samples
        foot = [*thirds(mean), *thirds(square - dose * mean)]
        foot = [jnp.concatenate([v, *gap], axis=1) for v in foot]
        part = dot0(left, right) + dot0(left_fix, right_fix)
        out_refs[k][:sub, :] = part.astype(BF16)
        out_refs[k][sub:, :] = stacked(col_rows + foot, 16).astype(BF16)


def more_tiles(left_ref, fix_ref, right, out_ref):
    n_rep, rows, _ = out_ref.shape
    sub, cols = rows - 8, right.shape[1]
    right_fix, col_rows = column_side(right)
    foot = stacked(col_rows, 8).astype(BF16)
    for q in range(n_rep):
        at = slice(q * sub, (q + 1) * sub)
        part = dot0(left_ref[:, at], right) + dot0(fix_ref[:, at], right_fix)
        out_ref[q, :sub, :cols] = part.astype(BF16)
        out_ref[q, sub:, :cols] = foot


def tile_second(first_col, left_ref, fix_ref, own_ref, out_ref):
    more_tiles(left_ref, fix_ref, own_ref[:, first_col : first_col + out_ref.shape[2]], out_ref)


def tile_third(left_ref, fix_ref, swapped_ref, *refs):
    *second, out_ref = refs
    samples, cols = left_ref.shape[0], swapped_ref.shape[2]
    for ref in second:
        out_ref[:, :, cols:] = ref[...]
    more_tiles(left_ref, fix_ref, swapped_ref[...].reshape(samples, cols), out_ref)


def whole(means, squares, samples):
    count = len(means)
    mean = sum(means) / count
    off = [m - mean for m in means]
    spread = sum(squares) / (count * samples) + sum(o * o for o in off) / count
    return off, lax.rsqrt(spread + EPS)


def three(s, i):
    return s[i : i + 1] + s[i + 1 : i + 2] + s[i + 2 : i + 3]


def joined(parts, stats, turned, samples):
    n_rep = len(parts)
    off, scale = whole([three(s, 0) for s in stats], [three(s, 3) for s in stats], samples)
    total = sum(p.astype(F32) for p in parts)
    for q in range(n_rep):
        total += (turned[:, q : q + 1] * samples) * off[q]
    return total * turned[:, n_rep : n_rep + 1] * scale


def join_first(samples, *refs):
    *in_refs, turned_ref, near_ref, half_ref = refs
    n_rep = len(in_refs)
    sub, near = near_ref.shape
    stats = [r[sub:, :].astype(F32) for r in in_refs]
    l_off, l_scale = whole(
        [three(s[:, :sub], 6) for s in stats], [three(s[:, :sub], 9) for s in stats], samples
    )
    l_scale = l_scale / (n_rep * samples)
    turned = stacked(l_off + [l_scale], 8).T
    total = joined([r[:sub, :] for r in in_refs], stats, turned, samples)
    near_ref[...] = total[:, :near]
    half_ref[...] = total[:, near:]
    group = lax.axis_index("rep")
    line = lax.broadcasted_iota(jnp.int32, (8, sub), 0)
    ordered = jnp.where(line == n_rep, l_scale, 0.0)
    for k in range(n_rep):
        ordered = jnp.where(line == lax.rem(group + n_rep - k, n_rep), l_off[k], ordered)
    turned_ref[...] = ordered.T


def join_second(samples, in_ref, turned_ref, near_ref, main_ref):
    n_rep, _, _ = in_ref.shape
    sub, width = main_ref.shape
    half, near = width // 2, near_ref.shape[1]
    core = lax.rem(lax.axis_index("col"), 2)
    stats = [in_ref[q, sub:, :].astype(F32) for q in range(n_rep)]
    total = joined([in_ref[q, :sub, :] for q in range(n_rep)], stats, turned_ref[...], samples)
    mine = pl.multiple_of(core * half, half)
    main_ref[:, pl.ds(pl.multiple_of((1 - core) * half, half), half)] = total[:, :half]
    if near < half:
        main_ref[:, pl.ds(mine, half - near)] = total[:, half:]
    main_ref[:, pl.ds(pl.multiple_of(mine + half - near, 128), near)] = near_ref[...]


def steps(genotypes):
    sample_rows, variants = genotypes.shape
    n_row, n_col, n_rep = (lax.axis_size(a) for a in ("row", "col", "rep"))
    width = variants // n_row
    half, slab = width // 2, width // n_col
    pairs = n_row * n_col
    samples = sample_rows * pairs
    sub = width // n_rep
    cols = half + slab
    near = NEAR * half // 4
    one, two = near + slab, width - near
    shape = jax.ShapeDtypeStruct

    payload = pl.pallas_call(
        functools.partial(pack_body, n_row, n_col),
        out_shape=shape((pairs, sample_rows, half + cols), BF16),
        compiler_params=params(8),
        cost_estimate=cost(0, 4 * pairs * sample_rows * (half + cols)),
        name="pack",
    )(genotypes)
    arrived = lax.all_to_all(payload, ("row", "col"), 0, 0, tiled=True)

    to_pair, to_core, own = pl.pallas_call(
        split_body,
        out_shape=(
            shape((pairs, sample_rows, half), BF16),
            shape((pairs, sample_rows, half), BF16),
            shape((samples, half + cols), BF16),
        ),
        compiler_params=params(8),
        cost_estimate=cost(0, 8 * samples * (half + cols)),
        name="split",
    )(arrived)

    def mate(r, c):
        return ((r - 1) % n_row) * n_col + c + 1 if c % 2 == 0 else ((r + 1) % n_row) * n_col + c - 1

    mates = [(r * n_col + c, mate(r, c)) for r in range(n_row) for c in range(n_col)]
    swapped = lax.ppermute(to_pair, ("row", "col"), mates)
    other = lax.ppermute(to_core, "col", [(c, c ^ 1) for c in range(n_col)])
    left, fix, *parts = pl.pallas_call(
        tile_first,
        out_shape=(
            shape((samples, width), BF16),
            shape((8, width), BF16),
            *[shape((sub + 16, one), BF16)] * n_rep,
        ),
        compiler_params=params(16),
        cost_estimate=cost(2 * samples * width * one, 2 * samples * (2 * width + one)),
        name="tile_first",
    )(own, other)
    for k in range(1, n_rep):
        parts[k] = lax.ppermute(parts[k], "rep", [(q, (q + k) % n_rep) for q in range(n_rep)])
    rest = half - near
    second = []
    if rest:
        second = [
            pl.pallas_call(
                functools.partial(tile_second, half),
                out_shape=shape((n_rep, sub + 8, rest), BF16),
                compiler_params=params(16),
                cost_estimate=cost(2 * samples * width * rest, 2 * samples * 2 * width),
                name="tile_second",
            )(left, fix, own)
        ]
    part_two = pl.pallas_call(
        tile_third,
        out_shape=shape((n_rep, sub + 8, two), BF16),
        compiler_params=params(16),
        cost_estimate=cost(2 * samples * width * half, 2 * samples * (width + half)),
        name="tile_third",
    )(left, fix, swapped, *second)
    got_two = lax.all_to_all(part_two, "rep", 0, 0, tiled=True)
    turned, near_main, far = pl.pallas_call(
        functools.partial(join_first, samples),
        out_shape=(shape((sub, 8), F32), shape((sub, near), F32), shape((sub, slab), F32)),
        compiler_params=params(8),
        cost_estimate=cost(12 * sub * one, 12 * sub * one),
        name="join_first",
    )(*parts)
    main = pl.pallas_call(
        functools.partial(join_second, samples),
        out_shape=shape((sub, width), F32),
        compiler_params=params(8),
        cost_estimate=cost(12 * sub * two, 12 * sub * two),
        name="join_second",
    )(got_two, turned, near_main)
    return main.reshape(1, 1, sub, width), far.reshape(1, sub, slab)


def solution(mesh):
    return jax.shard_map(
        steps,
        mesh=mesh,
        in_specs=(P(("row", "col", "rep"), None),),
        out_specs=(P("row", "col", "rep", None), P("row", "rep", "col")),
        check_vma=False,
    )
```

```python
import functools

import jax
import jax.numpy as jnp
from jax import lax
from jax.experimental import pallas as pl
from jax.experimental.pallas import tpu as pltpu
from jax.sharding import PartitionSpec as P


F32 = jnp.float32
BF16 = jnp.bfloat16
EPS = 1e-05


def params(mib):
    return pltpu.CompilerParams(vmem_limit_bytes=mib << 20)


def cost(flops, size):
    return pl.CostEstimate(flops=flops, bytes_accessed=size, transcendentals=0)


def thirds(v):
    hi = v.astype(BF16).astype(F32)
    rest = v - hi
    mid = rest.astype(BF16).astype(F32)
    return hi, mid, (rest - mid).astype(BF16).astype(F32)


def sums(v):
    v = v.astype(F32)
    return jnp.sum(v, axis=0, keepdims=True), jnp.sum(v * v, axis=0, keepdims=True)


def stacked(rows, count, held=None):
    gap = jnp.zeros((count - (held or len(rows)), rows[0].shape[1]), F32)
    return jnp.concatenate([*rows, gap], axis=0)


def dot0(a, b):
    return lax.dot_general(a, b, (((0,), (0,)), ((), ())), preferred_element_type=F32)


def pack_body(n_row, n_col, x_ref, out_ref):
    width = x_ref.shape[1] // n_row
    half, slab = width // 2, width // n_col
    for r in range(n_row):
        for c in range(n_col):
            d = r * n_col + c
            near = r * width + (c % 2) * half
            pair = ((r + c) % n_row) * width + (c % 2) * half
            far = ((r + n_row // 2) % n_row) * width + c * slab
            out_ref[d, :, :half] = x_ref[:, near : near + half]
            out_ref[d, :, half : 2 * half] = x_ref[:, pair : pair + half]
            out_ref[d, :, 2 * half :] = x_ref[:, far : far + slab]


def split_body(in_ref, pair_ref, core_ref, own_ref):
    half = pair_ref.shape[2]
    core_ref[...] = in_ref[:, :, :half]
    pair_ref[...] = in_ref[:, :, half : 2 * half]
    own_ref[...] = in_ref[...].reshape(own_ref.shape)


def column_side(right):
    samples = right.shape[0]
    dose, square = sums(right)
    hi, mid, lo = thirds(dose)
    fix = (stacked([hi, mid, hi, mid, lo, hi], 8) * (-1.0 / samples)).astype(BF16)
    mean = dose / samples
    return fix, [*thirds(mean), *thirds(square - dose * mean)]


def partners(group):
    return group, group + 1 - 2 * lax.rem(group, 2), 3 - group, lax.rem(group + 2, 4)


def piece(q, left_ref, right, right_fix, foot, out_ref):
    rows, cols = out_ref.shape
    sub, samples = rows - 16, left_ref.shape[0]
    left = left_ref[:, pl.ds(pl.multiple_of(q * sub, sub), sub)]
    dose, square = sums(left)
    hi, mid, lo = thirds(dose)
    left_fix = stacked([hi, hi, mid, mid, hi, lo], 8).astype(BF16)
    mean = dose / samples
    gap = jnp.zeros((1, cols - sub), F32)
    mine = [*thirds(mean), *thirds(square - dose * mean)]
    mine = [jnp.concatenate([v, gap], axis=1) for v in mine]
    part = dot0(left, right) + dot0(left_fix, right_fix)
    out_ref[:sub, :] = part.astype(BF16)
    out_ref[sub:, :] = stacked([foot[:6], *mine], 16, 12).astype(BF16)
    return left_fix


def tile_across(own_ref, other_ref, left_ref, fix_ref, right_fix_ref, foot_ref, out_ref):
    samples, half = own_ref.shape[0], other_ref.shape[2]
    core = lax.rem(lax.axis_index("col"), 2)
    left_ref[:, pl.ds(pl.multiple_of(core * half, half), half)] = own_ref[:, :half]
    left_ref[:, pl.ds(pl.multiple_of((1 - core) * half, half), half)] = other_ref[...].reshape(samples, half)
    right = own_ref[:, half:]
    right_fix, col_rows = column_side(right)
    foot = stacked(col_rows, 8)
    right_fix_ref[...] = right_fix
    foot_ref[...] = foot
    q = partners(lax.axis_index("rep"))[3]
    fix_ref[...] = piece(q, left_ref, right, right_fix, foot, out_ref)


def tile_others(left_ref, across_ref, right_fix_ref, foot_ref, own_ref, fix_ref, *out_refs):
    sub, half = across_ref.shape[1], left_ref.shape[1] // 2
    *near, opposite = partners(lax.axis_index("rep"))
    fix_ref[:, pl.ds(pl.multiple_of(opposite * sub, sub), sub)] = across_ref[...]
    right, right_fix, foot = own_ref[:, half:], right_fix_ref[...], foot_ref[...]
    for q, ref in zip((near[1], near[2], near[0]), (out_refs[1], out_refs[2], out_refs[0])):
        fix_ref[:, pl.ds(pl.multiple_of(q * sub, sub), sub)] = piece(q, left_ref, right, right_fix, foot, ref)


def tile_second(left_ref, fix_ref, swapped_ref, out_ref, held_ref, sems):
    n_rep, rows, cols = out_ref.shape
    sub, samples = rows - 8, left_ref.shape[0]
    right = swapped_ref[...].reshape(samples, cols)
    right_fix, col_rows = column_side(right)
    foot = stacked(col_rows, 8).astype(BF16)
    copies = []
    for q in range(n_rep):
        at = slice(q * sub, (q + 1) * sub)
        part = dot0(left_ref[:, at], right) + dot0(fix_ref[:, at], right_fix)
        held_ref[q, :sub, :] = part.astype(BF16)
        held_ref[q, sub:, :] = foot
        copies.append(pltpu.make_async_copy(held_ref.at[q], out_ref.at[q], sems.at[q]))
        copies[-1].start()
    for copy in copies:
        copy.wait()


def whole(means, squares, samples):
    count = len(means)
    mean = sum(means) / count
    off = [m - mean for m in means]
    spread = sum(squares) / (count * samples) + sum(o * o for o in off) / count
    return off, lax.rsqrt(spread + EPS)


def three(s, i):
    return s[i : i + 1] + s[i + 1 : i + 2] + s[i + 2 : i + 3]


def joined(parts, off, scale, turned, samples):
    n_rep = len(parts)
    total = sum(p.astype(F32) for p in parts)
    for q in range(n_rep):
        total += (turned[:, q : q + 1] * samples) * off[q]
    return total * turned[:, n_rep : n_rep + 1] * scale


def join_first(samples, *refs):
    *in_refs, turned_ref, main_ref, half_ref, near_ref, sem = refs
    sub, near = near_ref.shape
    n_rep = len(in_refs)
    stats = [r[sub:, :].astype(F32) for r in in_refs]
    l_off, l_scale = whole(
        [three(s[:, :sub], 6) for s in stats], [three(s[:, :sub], 9) for s in stats], samples
    )
    l_scale = l_scale / (n_rep * samples)
    turned = stacked(l_off + [l_scale], 8).T
    off, scale = whole([three(s, 0) for s in stats], [three(s, 3) for s in stats], samples)
    total = joined([r[:sub, :] for r in in_refs], off, scale, turned, samples)
    near_ref[...] = total[:, :near]
    core = lax.rem(lax.axis_index("col"), 2)
    to = pl.ds(pl.multiple_of(core * near, near), near)
    copy = pltpu.make_async_copy(near_ref, main_ref.at[:, to], sem)
    copy.start()
    half_ref[...] = total[:, near:]
    line = lax.broadcasted_iota(jnp.int32, (8, sub), 0)
    ordered = jnp.where(line == n_rep, l_scale, 0.0)
    for source, off in zip(partners(lax.axis_index("rep")), l_off):
        ordered = jnp.where(line == source, off, ordered)
    turned_ref[...] = ordered.T
    copy.wait()


def join_second(samples, in_ref, turned_ref, _, main_ref, held_ref, sems):
    n_rep, rows, half = in_ref.shape
    sub = rows - 8
    core = lax.rem(lax.axis_index("col"), 2)
    to = pl.ds(pl.multiple_of((1 - core) * half, half), half)
    stats = [in_ref[q, sub:, :].astype(F32) for q in range(n_rep)]
    off, scale = whole([three(s, 0) for s in stats], [three(s, 3) for s in stats], samples)
    pieces = sems.shape[0]
    step = sub // pieces
    copies = []
    for i in range(pieces):
        at = slice(i * step, (i + 1) * step)
        total = joined([in_ref[q, at, :] for q in range(n_rep)], off, scale, turned_ref[at, :], samples)
        held_ref[at, :] = total
        copies.append(pltpu.make_async_copy(held_ref.at[at, :], main_ref.at[at, to], sems.at[i]))
        copies[-1].start()
    for copy in copies:
        copy.wait()


def steps(genotypes):
    sample_rows, variants = genotypes.shape
    n_row, n_col, n_rep = (lax.axis_size(a) for a in ("row", "col", "rep"))
    width = variants // n_row
    half, slab = width // 2, width // n_col
    pairs = n_row * n_col
    samples = sample_rows * pairs
    sub = width // n_rep
    cols = half + slab
    shape = jax.ShapeDtypeStruct

    payload = pl.pallas_call(
        functools.partial(pack_body, n_row, n_col),
        out_shape=shape((pairs, sample_rows, half + cols), BF16),
        compiler_params=params(8),
        cost_estimate=cost(0, 4 * pairs * sample_rows * (half + cols)),
        name="pack",
    )(genotypes)
    arrived = lax.all_to_all(payload, ("row", "col"), 0, 0, tiled=True)

    to_pair, to_core, own = pl.pallas_call(
        split_body,
        out_shape=(
            shape((pairs, sample_rows, half), BF16),
            shape((pairs, sample_rows, half), BF16),
            shape((samples, half + cols), BF16),
        ),
        compiler_params=params(8),
        cost_estimate=cost(0, 8 * samples * (half + cols)),
        name="split",
    )(arrived)

    def mate(r, c):
        return ((r - 1) % n_row) * n_col + c + 1 if c % 2 == 0 else ((r + 1) % n_row) * n_col + c - 1

    mates = [(r * n_col + c, mate(r, c)) for r in range(n_row) for c in range(n_col)]
    swapped = lax.ppermute(to_pair, ("row", "col"), mates)
    other = lax.ppermute(to_core, "col", [(c, c ^ 1) for c in range(n_col)])
    left, across_fix, right_fix, foot, opposite = pl.pallas_call(
        tile_across,
        out_shape=(
            shape((samples, width), BF16),
            shape((8, sub), BF16),
            shape((8, cols), BF16),
            shape((8, cols), F32),
            shape((sub + 16, cols), BF16),
        ),
        compiler_params=params(16),
        cost_estimate=cost(2 * samples * sub * cols, 2 * samples * (2 * width + cols)),
        name="tile_across",
    )(own, other)
    opposite = lax.ppermute(opposite, "rep", [(q, (q + 2) % n_rep) for q in range(n_rep)])
    fix, *parts = pl.pallas_call(
        tile_others,
        out_shape=(shape((8, width), BF16), *[shape((sub + 16, cols), BF16)] * (n_rep - 1)),
        compiler_params=params(16),
        cost_estimate=cost(6 * samples * sub * cols, 2 * samples * (width + cols)),
        name="tile_others",
    )(left, across_fix, right_fix, foot, own)
    parts[1] = lax.ppermute(parts[1], "rep", [(q, q ^ 1) for q in range(n_rep)])
    parts[2] = lax.ppermute(parts[2], "rep", [(q, n_rep - 1 - q) for q in range(n_rep)])
    parts.append(opposite)
    partial = pl.pallas_call(
        tile_second,
        out_shape=shape((n_rep, sub + 8, half), BF16),
        out_specs=pl.BlockSpec(memory_space=pl.ANY),
        scratch_shapes=[pltpu.VMEM((n_rep, sub + 8, half), BF16), pltpu.SemaphoreType.DMA((n_rep,))],
        compiler_params=params(16),
        cost_estimate=cost(2 * samples * width * half, 2 * samples * (width + half)),
        name="tile_second",
    )(left, fix, swapped)
    got = lax.all_to_all(partial, "rep", 0, 0, tiled=True)
    vmem = pl.BlockSpec(memory_space=pltpu.VMEM)
    far_off = pl.BlockSpec(memory_space=pltpu.HBM)
    turned, main, far = pl.pallas_call(
        functools.partial(join_first, samples),
        out_shape=(shape((sub, 8), F32), shape((sub, width), F32), shape((sub, slab), F32)),
        out_specs=(vmem, far_off, vmem),
        scratch_shapes=[pltpu.VMEM((sub, half), F32), pltpu.SemaphoreType.DMA],
        compiler_params=params(8),
        cost_estimate=cost(12 * sub * cols, 12 * sub * cols),
        name="join_first",
    )(*parts)
    main = pl.pallas_call(
        functools.partial(join_second, samples),
        out_shape=shape((sub, width), F32),
        in_specs=[vmem, vmem, far_off],
        out_specs=far_off,
        scratch_shapes=[pltpu.VMEM((sub, half), F32), pltpu.SemaphoreType.DMA((4,))],
        input_output_aliases={2: 0},
        compiler_params=params(8),
        cost_estimate=cost(12 * sub * half, 12 * sub * half),
        name="join_second",
    )(got, turned, main)
    return main.reshape(1, 1, sub, width), far.reshape(1, sub, slab)


def solution(mesh):
    return jax.shard_map(
        steps,
        mesh=mesh,
        in_specs=(P(("row", "col", "rep"), None),),
        out_specs=(P("row", "col", "rep", None), P("row", "rep", "col")),
        check_vma=False,
    )
```

```python
import functools

import jax
import jax.numpy as jnp
from jax import lax
from jax.experimental import pallas as pl
from jax.experimental.pallas import tpu as pltpu
from jax.sharding import PartitionSpec as P


F32 = jnp.float32
BF16 = jnp.bfloat16
EPS = 1e-05


def params(mib):
    return pltpu.CompilerParams(vmem_limit_bytes=mib << 20)


def cost(flops, size):
    return pl.CostEstimate(flops=flops, bytes_accessed=size, transcendentals=0)


def thirds(v):
    hi = v.astype(BF16).astype(F32)
    rest = v - hi
    mid = rest.astype(BF16).astype(F32)
    return hi, mid, (rest - mid).astype(BF16).astype(F32)


def sums(v):
    v = v.astype(F32)
    return jnp.sum(v, axis=0, keepdims=True), jnp.sum(v * v, axis=0, keepdims=True)


def stacked(rows, count, held=None):
    gap = jnp.zeros((count - (held or len(rows)), rows[0].shape[1]), F32)
    return jnp.concatenate([*rows, gap], axis=0)


def dot0(a, b):
    return lax.dot_general(a, b, (((0,), (0,)), ((), ())), preferred_element_type=F32)


def pack_body(n_row, n_col, x_ref, out_ref):
    width = x_ref.shape[1] // n_row
    half, slab = width // 2, width // n_col
    for r in range(n_row):
        for c in range(n_col):
            d = r * n_col + c
            near = r * width + (c % 2) * half
            pair = ((r + c) % n_row) * width + (c % 2) * half
            far = ((r + n_row // 2) % n_row) * width + c * slab
            out_ref[d, :, :half] = x_ref[:, near : near + half]
            out_ref[d, :, half : 2 * half] = x_ref[:, pair : pair + half]
            out_ref[d, :, 2 * half :] = x_ref[:, far : far + slab]


def split_body(in_ref, pair_ref, core_ref, own_ref):
    half = pair_ref.shape[2]
    core_ref[...] = in_ref[:, :, :half]
    pair_ref[...] = in_ref[:, :, half : 2 * half]
    own_ref[...] = in_ref[...].reshape(own_ref.shape)


def column_side(right):
    samples = right.shape[0]
    dose, square = sums(right)
    hi, mid, lo = thirds(dose)
    fix = (stacked([hi, mid, hi, mid, lo, hi], 8) * (-1.0 / samples)).astype(BF16)
    mean = dose / samples
    return fix, [*thirds(mean), *thirds(square - dose * mean)]


def partners(group):
    return group, group + 1 - 2 * lax.rem(group, 2), 3 - group, lax.rem(group + 2, 4)


def piece(q, left_ref, right, right_fix, foot, out_ref):
    rows, cols = out_ref.shape
    sub, samples = rows - 16, left_ref.shape[0]
    left = left_ref[:, pl.ds(pl.multiple_of(q * sub, sub), sub)]
    dose, square = sums(left)
    hi, mid, lo = thirds(dose)
    left_fix = stacked([hi, hi, mid, mid, hi, lo], 8).astype(BF16)
    mean = dose / samples
    gap = jnp.zeros((1, cols - sub), F32)
    mine = [*thirds(mean), *thirds(square - dose * mean)]
    mine = [jnp.concatenate([v, gap], axis=1) for v in mine]
    part = dot0(left, right) + dot0(left_fix, right_fix)
    out_ref[:sub, :] = part.astype(BF16)
    out_ref[sub:, :] = stacked([foot[:6], *mine], 16, 12).astype(BF16)
    return left_fix


def tile_across(own_ref, other_ref, left_ref, fix_ref, right_fix_ref, foot_ref, out_ref):
    samples, half = own_ref.shape[0], other_ref.shape[2]
    core = lax.rem(lax.axis_index("col"), 2)
    left_ref[:, pl.ds(pl.multiple_of(core * half, half), half)] = own_ref[:, :half]
    left_ref[:, pl.ds(pl.multiple_of((1 - core) * half, half), half)] = other_ref[...].reshape(samples, half)
    right = own_ref[:, half:]
    right_fix, col_rows = column_side(right)
    foot = stacked(col_rows, 8)
    right_fix_ref[...] = right_fix
    foot_ref[...] = foot
    q = partners(lax.axis_index("rep"))[3]
    fix_ref[...] = piece(q, left_ref, right, right_fix, foot, out_ref)


def tile_near(left_ref, right_fix_ref, foot_ref, own_ref, fix_a_ref, fix_b_ref, a_ref, b_ref):
    half = left_ref.shape[1] // 2
    _, near_a, near_b, _ = partners(lax.axis_index("rep"))
    right, right_fix, foot = own_ref[:, half:], right_fix_ref[...], foot_ref[...]
    fix_a_ref[...] = piece(near_a, left_ref, right, right_fix, foot, a_ref)
    fix_b_ref[...] = piece(near_b, left_ref, right, right_fix, foot, b_ref)


def tile_self(left_ref, right_fix_ref, foot_ref, own_ref, a_ref, b_ref, c_ref, fix_ref, out_ref):
    sub, half = a_ref.shape[1], left_ref.shape[1] // 2
    mine, *others = partners(lax.axis_index("rep"))
    right, right_fix, foot = own_ref[:, half:], right_fix_ref[...], foot_ref[...]
    fixes = [piece(mine, left_ref, right, right_fix, foot, out_ref), a_ref[...], b_ref[...], c_ref[...]]
    for q, fix in zip((mine, *others), fixes):
        fix_ref[:, pl.ds(pl.multiple_of(q * sub, sub), sub)] = fix


def tile_second(left_ref, fix_ref, swapped_ref, out_ref, held_ref, sems):
    n_rep, rows, cols = out_ref.shape
    sub, samples = rows - 8, left_ref.shape[0]
    right = swapped_ref[...].reshape(samples, cols)
    right_fix, col_rows = column_side(right)
    foot = stacked(col_rows, 8).astype(BF16)
    copies = []
    for q in range(n_rep):
        at = slice(q * sub, (q + 1) * sub)
        part = dot0(left_ref[:, at], right) + dot0(fix_ref[:, at], right_fix)
        held_ref[q, :sub, :] = part.astype(BF16)
        held_ref[q, sub:, :] = foot
        copies.append(pltpu.make_async_copy(held_ref.at[q], out_ref.at[q], sems.at[q]))
        copies[-1].start()
    for copy in copies:
        copy.wait()


def whole(means, squares, samples):
    count = len(means)
    mean = sum(means) / count
    off = [m - mean for m in means]
    spread = sum(squares) / (count * samples) + sum(o * o for o in off) / count
    return off, lax.rsqrt(spread + EPS)


def three(s, i):
    return s[i : i + 1] + s[i + 1 : i + 2] + s[i + 2 : i + 3]


def joined(parts, off, scale, turned, samples):
    n_rep = len(parts)
    total = sum(p.astype(F32) for p in parts)
    for q in range(n_rep):
        total += (turned[:, q : q + 1] * samples) * off[q]
    return total * turned[:, n_rep : n_rep + 1] * scale


def join_first(samples, *refs):
    *in_refs, turned_ref, main_ref, half_ref, near_ref, sem = refs
    sub, near = near_ref.shape
    n_rep = len(in_refs)
    stats = [r[sub:, :].astype(F32) for r in in_refs]
    l_off, l_scale = whole(
        [three(s[:, :sub], 6) for s in stats], [three(s[:, :sub], 9) for s in stats], samples
    )
    l_scale = l_scale / (n_rep * samples)
    turned = stacked(l_off + [l_scale], 8).T
    off, scale = whole([three(s, 0) for s in stats], [three(s, 3) for s in stats], samples)
    total = joined([r[:sub, :] for r in in_refs], off, scale, turned, samples)
    near_ref[...] = total[:, :near]
    core = lax.rem(lax.axis_index("col"), 2)
    to = pl.ds(pl.multiple_of(core * near, near), near)
    copy = pltpu.make_async_copy(near_ref, main_ref.at[:, to], sem)
    copy.start()
    half_ref[...] = total[:, near:]
    line = lax.broadcasted_iota(jnp.int32, (8, sub), 0)
    ordered = jnp.where(line == n_rep, l_scale, 0.0)
    for source, off in zip(partners(lax.axis_index("rep")), l_off):
        ordered = jnp.where(line == source, off, ordered)
    turned_ref[...] = ordered.T
    copy.wait()


def join_second(samples, in_ref, turned_ref, _, main_ref, held_ref, sems):
    n_rep, rows, half = in_ref.shape
    sub = rows - 8
    core = lax.rem(lax.axis_index("col"), 2)
    to = pl.ds(pl.multiple_of((1 - core) * half, half), half)
    stats = [in_ref[q, sub:, :].astype(F32) for q in range(n_rep)]
    off, scale = whole([three(s, 0) for s in stats], [three(s, 3) for s in stats], samples)
    pieces = sems.shape[0]
    step = sub // pieces
    copies = []
    for i in range(pieces):
        at = slice(i * step, (i + 1) * step)
        total = joined([in_ref[q, at, :] for q in range(n_rep)], off, scale, turned_ref[at, :], samples)
        held_ref[at, :] = total
        copies.append(pltpu.make_async_copy(held_ref.at[at, :], main_ref.at[at, to], sems.at[i]))
        copies[-1].start()
    for copy in copies:
        copy.wait()


def steps(genotypes):
    sample_rows, variants = genotypes.shape
    n_row, n_col, n_rep = (lax.axis_size(a) for a in ("row", "col", "rep"))
    width = variants // n_row
    half, slab = width // 2, width // n_col
    pairs = n_row * n_col
    samples = sample_rows * pairs
    sub = width // n_rep
    cols = half + slab
    shape = jax.ShapeDtypeStruct

    payload = pl.pallas_call(
        functools.partial(pack_body, n_row, n_col),
        out_shape=shape((pairs, sample_rows, half + cols), BF16),
        compiler_params=params(8),
        cost_estimate=cost(0, 4 * pairs * sample_rows * (half + cols)),
        name="pack",
    )(genotypes)
    arrived = lax.all_to_all(payload, ("row", "col"), 0, 0, tiled=True)

    to_pair, to_core, own = pl.pallas_call(
        split_body,
        out_shape=(
            shape((pairs, sample_rows, half), BF16),
            shape((pairs, sample_rows, half), BF16),
            shape((samples, half + cols), BF16),
        ),
        compiler_params=params(8),
        cost_estimate=cost(0, 8 * samples * (half + cols)),
        name="split",
    )(arrived)

    def mate(r, c):
        return ((r - 1) % n_row) * n_col + c + 1 if c % 2 == 0 else ((r + 1) % n_row) * n_col + c - 1

    mates = [(r * n_col + c, mate(r, c)) for r in range(n_row) for c in range(n_col)]
    swapped = lax.ppermute(to_pair, ("row", "col"), mates)
    other = lax.ppermute(to_core, "col", [(c, c ^ 1) for c in range(n_col)])
    left, across_fix, right_fix, foot, opposite = pl.pallas_call(
        tile_across,
        out_shape=(
            shape((samples, width), BF16),
            shape((8, sub), BF16),
            shape((8, cols), BF16),
            shape((8, cols), F32),
            shape((sub + 16, cols), BF16),
        ),
        compiler_params=params(16),
        cost_estimate=cost(2 * samples * sub * cols, 2 * samples * (2 * width + cols)),
        name="tile_across",
    )(own, other)
    opposite = lax.ppermute(opposite, "rep", [(q, (q + 2) % n_rep) for q in range(n_rep)])
    fix_a, fix_b, near_a, near_b = pl.pallas_call(
        tile_near,
        out_shape=(*[shape((8, sub), BF16)] * 2, *[shape((sub + 16, cols), BF16)] * 2),
        compiler_params=params(16),
        cost_estimate=cost(4 * samples * sub * cols, 2 * samples * (width + cols)),
        name="tile_near",
    )(left, right_fix, foot, own)
    near_a = lax.ppermute(near_a, "rep", [(q, q ^ 1) for q in range(n_rep)])
    near_b = lax.ppermute(near_b, "rep", [(q, n_rep - 1 - q) for q in range(n_rep)])
    fix, mine = pl.pallas_call(
        tile_self,
        out_shape=(shape((8, width), BF16), shape((sub + 16, cols), BF16)),
        compiler_params=params(16),
        cost_estimate=cost(2 * samples * sub * cols, 2 * samples * (width + cols)),
        name="tile_self",
    )(left, right_fix, foot, own, fix_a, fix_b, across_fix)
    parts = [mine, near_a, near_b, opposite]
    partial = pl.pallas_call(
        tile_second,
        out_shape=shape((n_rep, sub + 8, half), BF16),
        out_specs=pl.BlockSpec(memory_space=pl.ANY),
        scratch_shapes=[pltpu.VMEM((n_rep, sub + 8, half), BF16), pltpu.SemaphoreType.DMA((n_rep,))],
        compiler_params=params(16),
        cost_estimate=cost(2 * samples * width * half, 2 * samples * (width + half)),
        name="tile_second",
    )(left, fix, swapped)
    got = lax.all_to_all(partial, "rep", 0, 0, tiled=True)
    vmem = pl.BlockSpec(memory_space=pltpu.VMEM)
    far_off = pl.BlockSpec(memory_space=pltpu.HBM)
    turned, main, far = pl.pallas_call(
        functools.partial(join_first, samples),
        out_shape=(shape((sub, 8), F32), shape((sub, width), F32), shape((sub, slab), F32)),
        out_specs=(vmem, far_off, vmem),
        scratch_shapes=[pltpu.VMEM((sub, half), F32), pltpu.SemaphoreType.DMA],
        compiler_params=params(8),
        cost_estimate=cost(12 * sub * cols, 12 * sub * cols),
        name="join_first",
    )(*parts)
    main = pl.pallas_call(
        functools.partial(join_second, samples),
        out_shape=shape((sub, width), F32),
        in_specs=[vmem, vmem, far_off],
        out_specs=far_off,
        scratch_shapes=[pltpu.VMEM((sub, half), F32), pltpu.SemaphoreType.DMA((4,))],
        input_output_aliases={2: 0},
        compiler_params=params(8),
        cost_estimate=cost(12 * sub * half, 12 * sub * half),
        name="join_second",
    )(got, turned, main)
    return main.reshape(1, 1, sub, width), far.reshape(1, sub, slab)


def solution(mesh):
    return jax.shard_map(
        steps,
        mesh=mesh,
        in_specs=(P(("row", "col", "rep"), None),),
        out_specs=(P("row", "col", "rep", None), P("row", "rep", "col")),
        check_vma=False,
    )
```

```python
import functools

import jax
import jax.numpy as jnp
from jax import lax
from jax.experimental import pallas as pl
from jax.experimental.pallas import tpu as pltpu
from jax.sharding import PartitionSpec as P


F32 = jnp.float32
BF16 = jnp.bfloat16
EPS = 1e-05


def params(mib):
    return pltpu.CompilerParams(vmem_limit_bytes=mib << 20)


def cost(flops, size):
    return pl.CostEstimate(flops=flops, bytes_accessed=size, transcendentals=0)


def thirds(v):
    hi = v.astype(BF16).astype(F32)
    rest = v - hi
    mid = rest.astype(BF16).astype(F32)
    return hi, mid, (rest - mid).astype(BF16).astype(F32)


def sums(v):
    v = v.astype(F32)
    return jnp.sum(v, axis=0, keepdims=True), jnp.sum(v * v, axis=0, keepdims=True)


def stacked(rows, count, held=None):
    gap = jnp.zeros((count - (held or len(rows)), rows[0].shape[1]), F32)
    return jnp.concatenate([*rows, gap], axis=0)


def dot0(a, b):
    return lax.dot_general(a, b, (((0,), (0,)), ((), ())), preferred_element_type=F32)


def pack_body(n_row, n_col, x_ref, out_ref):
    width = x_ref.shape[1] // n_row
    half, slab = width // 2, width // n_col
    for r in range(n_row):
        for c in range(n_col):
            d = r * n_col + c
            near = r * width + (c % 2) * half
            pair = ((r + c) % n_row) * width + (c % 2) * half
            far = ((r + n_row // 2) % n_row) * width + c * slab
            out_ref[d, :, :half] = x_ref[:, near : near + half]
            out_ref[d, :, half : 2 * half] = x_ref[:, pair : pair + half]
            out_ref[d, :, 2 * half :] = x_ref[:, far : far + slab]


def split_body(in_ref, pair_ref, core_ref, own_ref):
    half = pair_ref.shape[2]
    core_ref[...] = in_ref[:, :, :half]
    pair_ref[...] = in_ref[:, :, half : 2 * half]
    own_ref[...] = in_ref[...].reshape(own_ref.shape)


def column_side(right):
    samples = right.shape[0]
    dose, square = sums(right)
    hi, mid, lo = thirds(dose)
    fix = (stacked([hi, mid, hi, mid, lo, hi], 8) * (-1.0 / samples)).astype(BF16)
    mean = dose / samples
    return fix, [*thirds(mean), *thirds(square - dose * mean)]


def partners(group):
    return group, group + 1 - 2 * lax.rem(group, 2), 3 - group, lax.rem(group + 2, 4)


def piece(q, left_ref, right, right_fix, foot, out_ref):
    rows, cols = out_ref.shape
    sub, samples = rows - 8, left_ref.shape[0]
    left = left_ref[:, pl.ds(pl.multiple_of(q * sub, sub), sub)]
    dose, square = sums(left)
    hi, mid, lo = thirds(dose)
    left_fix = stacked([hi, hi, mid, mid, hi, lo], 8).astype(BF16)
    mean = dose / samples
    hi, mid, lo = thirds(mean)
    top, low, _ = thirds(square - dose * mean)
    rest = cols - 2 * sub
    mine = [
        jnp.concatenate([hi, mid, lo[:, :rest]], axis=1),
        jnp.concatenate([top, low, lo[:, sub - rest :]], axis=1),
    ]
    part = dot0(left, right) + dot0(left_fix, right_fix)
    out_ref[:sub, :] = part.astype(BF16)
    out_ref[sub:, :] = jnp.concatenate([foot[:6], *mine], axis=0).astype(BF16)
    return left_fix


def tile_across(own_ref, other_ref, left_ref, fix_ref, right_fix_ref, foot_ref, out_ref):
    samples, half = own_ref.shape[0], other_ref.shape[2]
    core = lax.rem(lax.axis_index("col"), 2)
    left_ref[:, pl.ds(pl.multiple_of(core * half, half), half)] = own_ref[:, :half]
    left_ref[:, pl.ds(pl.multiple_of((1 - core) * half, half), half)] = other_ref[...].reshape(samples, half)
    right = own_ref[:, half:]
    right_fix, col_rows = column_side(right)
    foot = stacked(col_rows, 8)
    right_fix_ref[...] = right_fix
    foot_ref[...] = foot
    q = partners(lax.axis_index("rep"))[3]
    fix_ref[...] = piece(q, left_ref, right, right_fix, foot, out_ref)


def tile_near(left_ref, right_fix_ref, foot_ref, own_ref, fix_a_ref, fix_b_ref, a_ref, b_ref):
    half = left_ref.shape[1] // 2
    _, near_a, near_b, _ = partners(lax.axis_index("rep"))
    right, right_fix, foot = own_ref[:, half:], right_fix_ref[...], foot_ref[...]
    fix_a_ref[...] = piece(near_a, left_ref, right, right_fix, foot, a_ref)
    fix_b_ref[...] = piece(near_b, left_ref, right, right_fix, foot, b_ref)


def tile_self(left_ref, right_fix_ref, foot_ref, own_ref, a_ref, b_ref, c_ref, fix_ref, out_ref):
    sub, half = a_ref.shape[1], left_ref.shape[1] // 2
    mine, *others = partners(lax.axis_index("rep"))
    right, right_fix, foot = own_ref[:, half:], right_fix_ref[...], foot_ref[...]
    fixes = [piece(mine, left_ref, right, right_fix, foot, out_ref), a_ref[...], b_ref[...], c_ref[...]]
    for q, fix in zip((mine, *others), fixes):
        fix_ref[:, pl.ds(pl.multiple_of(q * sub, sub), sub)] = fix


def tile_second(left_ref, fix_ref, swapped_ref, out_ref, held_ref, sems):
    n_rep, rows, cols = out_ref.shape
    sub, samples = rows - 8, left_ref.shape[0]
    right = swapped_ref[...].reshape(samples, cols)
    right_fix, col_rows = column_side(right)
    foot = stacked(col_rows, 8).astype(BF16)
    copies = []
    for q in range(n_rep):
        at = slice(q * sub, (q + 1) * sub)
        part = dot0(left_ref[:, at], right) + dot0(fix_ref[:, at], right_fix)
        held_ref[q, :sub, :] = part.astype(BF16)
        held_ref[q, sub:, :] = foot
        copies.append(pltpu.make_async_copy(held_ref.at[q], out_ref.at[q], sems.at[q]))
        copies[-1].start()
    for copy in copies:
        copy.wait()


def whole(means, squares, samples):
    count = len(means)
    mean = sum(means) / count
    off = [m - mean for m in means]
    spread = sum(squares) / (count * samples) + sum(o * o for o in off) / count
    return off, lax.rsqrt(spread + EPS)


def three(s, i):
    return s[i : i + 1] + s[i + 1 : i + 2] + s[i + 2 : i + 3]


def joined(parts, off, scale, turned, samples):
    n_rep = len(parts)
    total = sum(p.astype(F32) for p in parts)
    for q in range(n_rep):
        total += (turned[:, q : q + 1] * samples) * off[q]
    return total * turned[:, n_rep : n_rep + 1] * scale


def join_first(samples, *refs):
    *in_refs, turned_ref, main_ref, half_ref, near_ref, sem = refs
    sub, near = near_ref.shape
    n_rep = len(in_refs)
    stats = [r[sub:, :].astype(F32) for r in in_refs]
    last = [jnp.concatenate([s[6:7, 2 * sub :], s[7:8, 2 * sub :]], axis=1) for s in stats]
    pair = lambda s, i: s[i : i + 1, :sub] + s[i : i + 1, sub : 2 * sub]
    l_mean = [pair(s, 6) + v for s, v in zip(stats, last)]
    l_off, l_scale = whole(l_mean, [pair(s, 7) for s in stats], samples)
    l_scale = l_scale / (n_rep * samples)
    turned = stacked(l_off + [l_scale], 8).T
    off, scale = whole([three(s, 0) for s in stats], [three(s, 3) for s in stats], samples)
    total = joined([r[:sub, :] for r in in_refs], off, scale, turned, samples)
    near_ref[...] = total[:, :near]
    core = lax.rem(lax.axis_index("col"), 2)
    to = pl.ds(pl.multiple_of(core * near, near), near)
    copy = pltpu.make_async_copy(near_ref, main_ref.at[:, to], sem)
    copy.start()
    half_ref[...] = total[:, near:]
    line = lax.broadcasted_iota(jnp.int32, (8, sub), 0)
    ordered = jnp.where(line == n_rep, l_scale, 0.0)
    for source, off in zip(partners(lax.axis_index("rep")), l_off):
        ordered = jnp.where(line == source, off, ordered)
    turned_ref[...] = ordered.T
    copy.wait()


def join_second(samples, in_ref, turned_ref, _, main_ref, held_ref, sems):
    n_rep, rows, half = in_ref.shape
    sub = rows - 8
    core = lax.rem(lax.axis_index("col"), 2)
    to = pl.ds(pl.multiple_of((1 - core) * half, half), half)
    stats = [in_ref[q, sub:, :].astype(F32) for q in range(n_rep)]
    off, scale = whole([three(s, 0) for s in stats], [three(s, 3) for s in stats], samples)
    pieces = sems.shape[0]
    step = sub // pieces
    copies = []
    for i in range(pieces):
        at = slice(i * step, (i + 1) * step)
        total = joined([in_ref[q, at, :] for q in range(n_rep)], off, scale, turned_ref[at, :], samples)
        held_ref[at, :] = total
        copies.append(pltpu.make_async_copy(held_ref.at[at, :], main_ref.at[at, to], sems.at[i]))
        copies[-1].start()
    for copy in copies:
        copy.wait()


def steps(genotypes):
    sample_rows, variants = genotypes.shape
    n_row, n_col, n_rep = (lax.axis_size(a) for a in ("row", "col", "rep"))
    width = variants // n_row
    half, slab = width // 2, width // n_col
    pairs = n_row * n_col
    samples = sample_rows * pairs
    sub = width // n_rep
    cols = half + slab
    shape = jax.ShapeDtypeStruct

    payload = pl.pallas_call(
        functools.partial(pack_body, n_row, n_col),
        out_shape=shape((pairs, sample_rows, half + cols), BF16),
        compiler_params=params(8),
        cost_estimate=cost(0, 4 * pairs * sample_rows * (half + cols)),
        name="pack",
    )(genotypes)
    arrived = lax.all_to_all(payload, ("row", "col"), 0, 0, tiled=True)

    to_pair, to_core, own = pl.pallas_call(
        split_body,
        out_shape=(
            shape((pairs, sample_rows, half), BF16),
            shape((pairs, sample_rows, half), BF16),
            shape((samples, half + cols), BF16),
        ),
        compiler_params=params(8),
        cost_estimate=cost(0, 8 * samples * (half + cols)),
        name="split",
    )(arrived)

    def mate(r, c):
        return ((r - 1) % n_row) * n_col + c + 1 if c % 2 == 0 else ((r + 1) % n_row) * n_col + c - 1

    mates = [(r * n_col + c, mate(r, c)) for r in range(n_row) for c in range(n_col)]
    swapped = lax.ppermute(to_pair, ("row", "col"), mates)
    other = lax.ppermute(to_core, "col", [(c, c ^ 1) for c in range(n_col)])
    left, across_fix, right_fix, foot, opposite = pl.pallas_call(
        tile_across,
        out_shape=(
            shape((samples, width), BF16),
            shape((8, sub), BF16),
            shape((8, cols), BF16),
            shape((8, cols), F32),
            shape((sub + 8, cols), BF16),
        ),
        compiler_params=params(16),
        cost_estimate=cost(2 * samples * sub * cols, 2 * samples * (2 * width + cols)),
        name="tile_across",
    )(own, other)
    opposite = lax.ppermute(opposite, "rep", [(q, (q + 2) % n_rep) for q in range(n_rep)])
    fix_a, fix_b, near_a, near_b = pl.pallas_call(
        tile_near,
        out_shape=(*[shape((8, sub), BF16)] * 2, *[shape((sub + 8, cols), BF16)] * 2),
        compiler_params=params(16),
        cost_estimate=cost(4 * samples * sub * cols, 2 * samples * (width + cols)),
        name="tile_near",
    )(left, right_fix, foot, own)
    near_a = lax.ppermute(near_a, "rep", [(q, q ^ 1) for q in range(n_rep)])
    near_b = lax.ppermute(near_b, "rep", [(q, n_rep - 1 - q) for q in range(n_rep)])
    fix, mine = pl.pallas_call(
        tile_self,
        out_shape=(shape((8, width), BF16), shape((sub + 8, cols), BF16)),
        compiler_params=params(16),
        cost_estimate=cost(2 * samples * sub * cols, 2 * samples * (width + cols)),
        name="tile_self",
    )(left, right_fix, foot, own, fix_a, fix_b, across_fix)
    parts = [mine, near_a, near_b, opposite]
    partial = pl.pallas_call(
        tile_second,
        out_shape=shape((n_rep, sub + 8, half), BF16),
        out_specs=pl.BlockSpec(memory_space=pl.ANY),
        scratch_shapes=[pltpu.VMEM((n_rep, sub + 8, half), BF16), pltpu.SemaphoreType.DMA((n_rep,))],
        compiler_params=params(16),
        cost_estimate=cost(2 * samples * width * half, 2 * samples * (width + half)),
        name="tile_second",
    )(left, fix, swapped)
    got = lax.all_to_all(partial, "rep", 0, 0, tiled=True)
    vmem = pl.BlockSpec(memory_space=pltpu.VMEM)
    far_off = pl.BlockSpec(memory_space=pltpu.HBM)
    turned, main, far = pl.pallas_call(
        functools.partial(join_first, samples),
        out_shape=(shape((sub, 8), F32), shape((sub, width), F32), shape((sub, slab), F32)),
        out_specs=(vmem, far_off, vmem),
        scratch_shapes=[pltpu.VMEM((sub, half), F32), pltpu.SemaphoreType.DMA],
        compiler_params=params(8),
        cost_estimate=cost(12 * sub * cols, 12 * sub * cols),
        name="join_first",
    )(*parts)
    main = pl.pallas_call(
        functools.partial(join_second, samples),
        out_shape=shape((sub, width), F32),
        in_specs=[vmem, vmem, far_off],
        out_specs=far_off,
        scratch_shapes=[pltpu.VMEM((sub, half), F32), pltpu.SemaphoreType.DMA((4,))],
        input_output_aliases={2: 0},
        compiler_params=params(8),
        cost_estimate=cost(12 * sub * half, 12 * sub * half),
        name="join_second",
    )(got, turned, main)
    return main.reshape(1, 1, sub, width), far.reshape(1, sub, slab)


def solution(mesh):
    return jax.shard_map(
        steps,
        mesh=mesh,
        in_specs=(P(("row", "col", "rep"), None),),
        out_specs=(P("row", "col", "rep", None), P("row", "rep", "col")),
        check_vma=False,
    )
```
